32 devices in a mesh: freq: 4 (over z), tile: 8 (over y, x, core).
Axes of the slice: x: 2, y: 2, z: 4, core: 2. Of those that a mesh axis runs over, the one named last changes fastest.
Arguments:
- signal: bfloat16 [4, 2, 128, 4096], P('freq', None, None, 'tile'), may hold values from -6 to 6
- v_factors: bfloat16 [4, 16, 2, 48, 4096], P('freq', None, None, None, 'tile'), may hold values from -0.375 to 0.375
- u_factors: bfloat16 [4, 16, 2, 48, 4096], P('freq', None, None, None, 'tile'), may hold values from -0.109375 to 0.109375
- tile_ranks: int32 [4, 16, 16], P('freq'), may hold values from 16 to 48
- row_order: int32 [16], replicated, may hold values from 0 to 15, each once
- col_order: int32 [16], replicated, may hold values from 0 to 15, each once
- time_gate: float32 [2, 4, 4], replicated, may hold values from -2 to 2
Outputs:
- forward_data: bfloat16 [4, 2, 128, 4096], P('freq', None, None, 'tile')
- adjoint_data: bfloat16 [4, 2, 128, 4096], P('freq', None, None, 'tile')
The draws below stay inside these ranges and needn't reach their ends.
Inputs may be any that keep to these rules, and one draw needn't show every extreme that they name: tile_ranks[f, i, j] is the rank of kernel tile (i, j) at frequency f. `row_order`: a permutation of the 16 kernel tile rows. `col_order`: a permutation of the 16 kernel tile columns.
All inputs are finite; a program needn't handle non-finite values.
Results may differ from the reference program's by a relative error of at most 0.0075.
Values may be sent and summed in bfloat16 or wider, within the bound.
No kernel may reach another device: no remote copies, remote signals or barrier semaphores. Data moves between devices by JAX's collectives and lax.ppermute only.
A program may use at most 128 MiB of HBM per device.

```python
import jax
import jax.numpy as jnp
from jax import lax

TILE = 256
RMAX = 48
RMIN = 16
SRC = 128
TR = 16
TC = 16
M = 4096
N = 4096
FREQS = 4


def with_ends(array, key, least, top_value):
    place = [jax.random.randint(jax.random.fold_in(key, axis), (), 0, length) for axis, length in enumerate(array.shape)]
    longest = array.shape.index(max(array.shape))
    neighbour = place[:longest] + [(place[longest] + 1) % array.shape[longest]] + place[longest + 1:]
    return array.at[tuple(place)].set(least).at[tuple(neighbour)].set(top_value)


def level_of(stream_key, extent, pieces, low, high):
    def one(dim, shards_of):
        steps = jax.random.uniform(jax.random.fold_in(jax.random.fold_in(stream_key, 6), dim), (shards_of,), jnp.float32, low / len(pieces), high / len(pieces))
        return jnp.repeat(jnp.exp(steps), extent[dim] // shards_of).reshape((-1,) + (1,) * (len(extent) - dim - 1))

    gain = one(*pieces[0])
    for cut in pieces[1:]:
        gain = gain * one(*cut)
    return gain


def gaussian(own_key, dims, width, most, split=(), held_as=jnp.bfloat16):
    values = jax.random.normal(own_key, dims, jnp.float32) * width
    if len(split) > 0:
        values = level_of(own_key, dims, split, -0.22, 0.18) * values
    return jnp.clip(values, min=-most, max=most).astype(held_as)


def setup_inputs(seed: int = 0) -> dict:
    key_list = jax.random.split(jax.random.key(seed), 8)
    return {
        "signal": gaussian(key_list[0], (FREQS, 2, SRC, N), 1.0, 6.0, ((0, 4), (3, 8))),
        "v_factors": gaussian(key_list[1], (FREQS, TR, 2, RMAX, N), TILE ** -0.5, 0.375, ((0, 4), (4, 8))),
        "u_factors": gaussian(key_list[2], (FREQS, TC, 2, RMAX, M), (4 * TC * RMAX) ** -0.5, 0.109375, ((0, 4), (4, 8))),
        "tile_ranks": with_ends(jax.random.randint(key_list[3], (FREQS, TR, TC), RMIN, RMAX + 1), jax.random.fold_in(key_list[3], 1), RMIN, RMAX).astype(jnp.int32),
        "row_order": jax.random.permutation(key_list[4], TR).astype(jnp.int32),
        "col_order": jax.random.permutation(key_list[5], TC).astype(jnp.int32),
        "time_gate": gaussian(key_list[6], (2, FREQS, FREQS), (2 * FREQS) ** -0.5, 2.0, (), jnp.float32),
    }


def combine(product, conjugate, stack_axis):
    if conjugate:
        real_part = product[0, 0] + product[1, 1]
        imag_part = product[0, 1] - product[1, 0]
    else:
        real_part = product[0, 0] - product[1, 1]
        imag_part = product[0, 1] + product[1, 0]
    return jnp.stack([real_part, imag_part], axis=stack_axis)


def reference(signal, v_factors, u_factors, tile_ranks, row_order, col_order, time_gate):
    stored = tile_ranks[:, row_order][:, :, col_order]
    rank_slots = jnp.arange(RMAX, dtype=jnp.int32)

    def forward_one(inputs):
        sig, right, left, ranks_here = inputs
        live_mask = (rank_slots[None, None, :] < ranks_here[:, :, None]).astype(jnp.float32)
        right_full = right.astype(jnp.float32).reshape(TR, 2, RMAX, TC, TILE)
        sources = sig.astype(jnp.float32).reshape(2, SRC, TC, TILE)
        product = jnp.einsum('kprlt,qslt->pqklrs', right_full, sources)
        coefficients = (combine(product, False, 0) * live_mask[None, :, :, :, None]).astype(jnp.bfloat16)
        left_full = left.astype(jnp.float32).reshape(TC, 2, RMAX, TR, TILE)
        product = jnp.einsum('lqrkt,pklrs->qpskt', left_full, coefficients.astype(jnp.float32))
        return combine(product, False, 0).reshape(2, SRC, M).astype(jnp.bfloat16)

    forward_all = lax.map(forward_one, (signal, v_factors, u_factors, stored))
    product = jnp.einsum('pfe,eqsm->pqfsm', time_gate, forward_all.astype(jnp.float32),
                         precision=lax.Precision.HIGHEST)
    gated_all = combine(product, False, 1).astype(jnp.bfloat16)

    def adjoint_one(inputs):
        gated_rows, right, left, ranks_here = inputs
        live_mask = (rank_slots[None, None, :] < ranks_here[:, :, None]).astype(jnp.float32)
        left_full = left.astype(jnp.float32).reshape(TC, 2, RMAX, TR, TILE)
        rows_here = gated_rows.astype(jnp.float32).reshape(2, SRC, TR, TILE)
        product = jnp.einsum('lqrkt,pskt->qpklrs', left_full, rows_here)
        adjoint_coef = (combine(product, True, 0) * live_mask[None, :, :, :, None]).astype(jnp.bfloat16)
        right_full = right.astype(jnp.float32).reshape(TR, 2, RMAX, TC, TILE)
        product = jnp.einsum('kqrlt,pklrs->qpslt', right_full, adjoint_coef.astype(jnp.float32))
        return combine(product, True, 0).reshape(2, SRC, N).astype(jnp.bfloat16)

    adjoint_all = lax.map(adjoint_one, (gated_all, v_factors, u_factors, stored))
    return forward_all, adjoint_all
```

```python
import functools

import jax
import jax.numpy as jnp
from jax import lax
from jax.experimental import pallas as pl
from jax.experimental.pallas import tpu as pltpu
from jax.sharding import PartitionSpec as P


F32 = jnp.float32
BF16 = jnp.bfloat16
VMEM = pl.BlockSpec(memory_space=pltpu.VMEM)
SMEM = pl.BlockSpec(memory_space=pltpu.SMEM)
NT = (((1,), (1,)), ((), ()))


def partner_order(count):
    return sorted(range(1, count), key=lambda d: (d == 1, bin(d >> 1).count("1"), d & 1, d))


def exchange(blocks, axis, order):
    count = lax.axis_size(axis)
    got = [None] * count
    got[0] = blocks[0]
    for d in order:
        got[d] = lax.ppermute(blocks[d], axis, [(i, i ^ d) for i in range(count)])
    return got


def analysis_kernel(dims, ranks_ref, rows_ref, cols_ref, factors_ref, *refs):
    tile_count, outer, inner, rank_most, width, sources, conjugate = dims
    per_dev = outer // tile_count
    spectra_refs = refs[: -tile_count - 2]
    out_refs = refs[-tile_count - 2 : -2]
    weights, held = refs[-2:]
    me = lax.axis_index("tile")
    if len(spectra_refs) == 1:
        real = spectra_refs[0][0]
        imag = spectra_refs[0][1]
        store = [(slice(None), real, imag)]
    else:
        group = lax.axis_index("freq")
        share = sources // len(spectra_refs)
        store = []
        for d, ref in enumerate(spectra_refs):
            place = pl.multiple_of((group ^ d) * share, share)
            store.append((pl.ds(place, share), ref[0], ref[1]))
    for where, real, imag in store:
        weights[0, 0, where] = real
        weights[0, 1, where] = imag
        weights[1, 0, where] = imag if conjugate else -imag
        weights[1, 1, where] = -real if conjugate else real
    slots = lax.broadcasted_iota(jnp.int32, (rank_most, 2 * sources), 0)
    for b in range(inner):
        span = slice(b * width, (b + 1) * width)
        w_real = weights[0, :, :, span].reshape(2 * sources, width)
        w_imag = weights[1, :, :, span].reshape(2 * sources, width)
        here = me * inner + b

        def group_of(start, size):
            f_real = factors_ref[pl.ds(start, size), 0, :, span].reshape(size * rank_most, width)
            f_imag = factors_ref[pl.ds(start, size), 1, :, span].reshape(size * rank_most, width)
            total = lax.dot_general(f_real, w_real, NT, preferred_element_type=F32)
            total += lax.dot_general(f_imag, w_imag, NT, preferred_element_type=F32)
            for a in range(size):
                if conjugate:
                    live = ranks_ref[rows_ref[here], cols_ref[start + a]]
                else:
                    live = ranks_ref[rows_ref[start + a], cols_ref[here]]
                part = total[a * rank_most : (a + 1) * rank_most]
                held[start + a, b] = jnp.where(slots < live, part, 0.0).astype(BF16)

        size = min(outer, 16)
        if outer == size:
            group_of(0, size)
        else:
            lax.fori_loop(0, outer // size, lambda g, c: (group_of(g * size, size), c)[1], 0)
    for d in range(tile_count):
        block = held[pl.ds((me ^ d) * per_dev, per_dev)]
        for b in range(inner):
            for a in range(per_dev):
                out_refs[d][a, b] = block[a, b]


def synthesis_kernel(dims, factors_ref, *refs):
    tile_count, outer, inner, rank_most, width, sources, conjugate, split = dims
    per_dev = outer // tile_count
    in_refs = refs[:tile_count]
    out_ref = refs[tile_count]
    split_refs = refs[tile_count + 1 : -1]
    held = refs[-1]
    me = lax.axis_index("tile")
    rows = per_dev * rank_most
    for d in range(tile_count):
        place = pl.multiple_of((me ^ d) * rows, rows)
        for b in range(inner):
            held[b, pl.ds(place, rows)] = in_refs[d][b].reshape(rows, 2 * sources)
    for b in range(inner):
        span = slice(b * width, (b + 1) * width)
        turned = held[b].T
        by_real = jnp.dot(
            turned,
            factors_ref[:, 0, :, span].reshape(outer * rank_most, width),
            preferred_element_type=F32,
        )
        by_imag = jnp.dot(
            turned,
            factors_ref[:, 1, :, span].reshape(outer * rank_most, width),
            preferred_element_type=F32,
        )
        if conjugate:
            real = by_real[:sources] + by_imag[sources:]
            imag = by_real[sources:] - by_imag[:sources]
        else:
            real = by_real[:sources] - by_imag[sources:]
            imag = by_real[sources:] + by_imag[:sources]
        out_ref[0, :, span] = real.astype(BF16)
        out_ref[1, :, span] = imag.astype(BF16)
    if split > 1:
        group = lax.axis_index("freq")
        share = sources // split
        for d in range(split):
            place = pl.multiple_of((group ^ d) * share, share)
            split_refs[d][...] = out_ref[:, pl.ds(place, share)]


def gate_kernel(freqs, gate_ref, *refs):
    in_refs, out_refs = refs[:freqs], refs[freqs:]
    group = lax.axis_index("freq")
    parts = [(ref[0].astype(F32), ref[1].astype(F32)) for ref in in_refs]
    for d in range(freqs):
        target = group ^ d
        real = imag = None
        for e, (x, y) in enumerate(parts):
            g = gate_ref[0, target, group ^ e]
            h = gate_ref[1, target, group ^ e]
            first = g * x - h * y
            second = g * y + h * x
            real = first if real is None else real + first
            imag = second if imag is None else imag + second
        out_refs[d][0] = real.astype(BF16)
        out_refs[d][1] = imag.astype(BF16)


def call(kernel, out_shape, specs, scratch, args, flops):
    held = sum(a.size * a.dtype.itemsize for a in args)
    held += sum(o.size * o.dtype.itemsize for o in out_shape)
    return pl.pallas_call(
        kernel,
        out_shape=out_shape,
        in_specs=specs,
        out_specs=[VMEM] * len(out_shape),
        scratch_shapes=scratch,
        cost_estimate=pl.CostEstimate(flops=flops, bytes_accessed=held, transcendentals=0),
    )(*args)


def shards(signal, v_factors, u_factors, tile_ranks, row_order, col_order, time_gate):
    tile_count = lax.axis_size("tile")
    freqs = lax.axis_size("freq")
    row_tiles, _, rank_most, col_local = v_factors.shape[1:]
    col_tiles = u_factors.shape[1]
    row_local = u_factors.shape[4]
    sources = signal.shape[2]
    col_dev = col_tiles // tile_count
    row_dev = row_tiles // tile_count
    width = col_local // col_dev
    share = sources // freqs
    flops = 8 * row_tiles * col_dev * rank_most * width * sources
    right, left = v_factors[0], u_factors[0]
    ranks = tile_ranks[0]
    tile_order = partner_order(tile_count)
    freq_order = list(range(freqs - 1, 0, -1))

    def analysis(factors, spectra, outer, inner, conjugate):
        per_dev = outer // tile_count
        dims = (tile_count, outer, inner, rank_most, width, sources, conjugate)
        block = jax.ShapeDtypeStruct((per_dev, inner, rank_most, 2 * sources), BF16)
        return call(
            functools.partial(analysis_kernel, dims),
            [block] * tile_count,
            [SMEM] * 3 + [VMEM] * (1 + len(spectra)),
            [
                pltpu.VMEM((2, 2, sources, inner * width), BF16),
                pltpu.VMEM((outer, inner, rank_most, 2 * sources), BF16),
            ],
            (ranks, row_order, col_order, factors, *spectra),
            flops,
        )

    def synthesis(factors, blocks, outer, inner, conjugate, split):
        dims = (tile_count, outer, inner, rank_most, width, sources, conjugate, split)
        shapes = [jax.ShapeDtypeStruct((2, sources, inner * width), BF16)]
        if split > 1:
            shapes += [jax.ShapeDtypeStruct((2, sources // split, inner * width), BF16)] * split
        return call(
            functools.partial(synthesis_kernel, dims),
            shapes,
            [VMEM] * (1 + tile_count),
            [pltpu.VMEM((inner, outer * rank_most, 2 * sources), BF16)],
            (factors, *blocks),
            flops,
        )

    sent = analysis(right, (signal[0],), row_tiles, col_dev, False)
    got = exchange(sent, "tile", tile_order)
    forward, *pieces = synthesis(left, got, col_tiles, row_dev, False, freqs)
    pieces = exchange(pieces, "freq", freq_order)
    gated = call(
        functools.partial(gate_kernel, freqs),
        [jax.ShapeDtypeStruct((2, share, row_local), BF16)] * freqs,
        [SMEM] + [VMEM] * freqs,
        [],
        (time_gate, *pieces),
        16 * freqs * freqs * share * row_local,
    )
    gated = exchange(gated, "freq", freq_order)
    sent = analysis(left, tuple(gated), col_tiles, row_dev, True)
    got = exchange(sent, "tile", tile_order)
    (adjoint,) = synthesis(right, got, row_tiles, col_dev, True, 1)
    return forward[None], adjoint[None]


def solution(mesh):
    return jax.shard_map(
        shards,
        mesh=mesh,
        in_specs=(
            P("freq", None, None, "tile"),
            P("freq", None, None, None, "tile"),
            P("freq", None, None, None, "tile"),
            P("freq", None, None),
            P(),
            P(),
            P(),
        ),
        out_specs=(P("freq", None, None, "tile"), P("freq", None, None, "tile")),
        check_vma=False,
    )
```

```python
import functools

import jax
import jax.numpy as jnp
from jax import lax
from jax.experimental import pallas as pl
from jax.experimental.pallas import tpu as pltpu
from jax.sharding import PartitionSpec as P


F32 = jnp.float32
BF16 = jnp.bfloat16
VMEM = pl.BlockSpec(memory_space=pltpu.VMEM)
SMEM = pl.BlockSpec(memory_space=pltpu.SMEM)
NT = (((1,), (1,)), ((), ()))


def partner_order(count):
    return sorted(range(1, count), key=lambda d: (d == 1, bin(d >> 1).count("1"), d & 1, d))


def exchange(blocks, axis, order):
    count = lax.axis_size(axis)
    got = [None] * count
    got[0] = blocks[0]
    for d in order:
        got[d] = lax.ppermute(blocks[d], axis, [(i, i ^ d) for i in range(count)])
    return got


def analysis_kernel(dims, ranks_ref, rows_ref, cols_ref, factors_ref, *refs):
    tile_count, outer, inner, rank_most, width, sources, conjugate = dims
    per_dev = outer // tile_count
    spectra_refs = refs[: -tile_count - 2]
    out_refs = refs[-tile_count - 2 : -2]
    weights, held = refs[-2:]
    me = lax.axis_index("tile")
    if len(spectra_refs) == 1:
        real = spectra_refs[0][0]
        imag = spectra_refs[0][1]
        store = [(slice(None), real, imag)]
    else:
        group = lax.axis_index("freq")
        share = sources // len(spectra_refs)
        store = []
        for d, ref in enumerate(spectra_refs):
            place = pl.multiple_of((group ^ d) * share, share)
            store.append((pl.ds(place, share), ref[0], ref[1]))
    for where, real, imag in store:
        weights[0, 0, where] = real
        weights[0, 1, where] = imag
        weights[1, 0, where] = imag if conjugate else -imag
        weights[1, 1, where] = -real if conjugate else real
    slots = lax.broadcasted_iota(jnp.int32, (rank_most, 2 * sources), 0)
    for b in range(inner):
        span = slice(b * width, (b + 1) * width)
        w_real = weights[0, :, :, span].reshape(2 * sources, width)
        w_imag = weights[1, :, :, span].reshape(2 * sources, width)
        here = me * inner + b

        def group_of(start, size):
            f_real = factors_ref[pl.ds(start, size), 0, :, span].reshape(size * rank_most, width)
            f_imag = factors_ref[pl.ds(start, size), 1, :, span].reshape(size * rank_most, width)
            total = lax.dot_general(f_real, w_real, NT, preferred_element_type=F32)
            total += lax.dot_general(f_imag, w_imag, NT, preferred_element_type=F32)
            for a in range(size):
                if conjugate:
                    live = ranks_ref[rows_ref[here], cols_ref[start + a]]
                else:
                    live = ranks_ref[rows_ref[start + a], cols_ref[here]]
                part = total[a * rank_most : (a + 1) * rank_most]
                held[start + a, b] = jnp.where(slots < live, part, 0.0).astype(BF16)

        size = min(outer, 16)
        if outer == size:
            group_of(0, size)
        else:
            lax.fori_loop(0, outer // size, lambda g, c: (group_of(g * size, size), c)[1], 0)
    for d in range(tile_count):
        block = held[pl.ds((me ^ d) * per_dev, per_dev)]
        for b in range(inner):
            for a in range(per_dev):
                out_refs[d][a, b] = block[a, b]


def synthesis_kernel(dims, factors_ref, *refs):
    tile_count, outer, inner, rank_most, width, sources, conjugate, split = dims
    per_dev = outer // tile_count
    in_refs = refs[:tile_count]
    out_ref = refs[tile_count]
    split_refs = refs[tile_count + 1 : -1]
    held = refs[-1]
    me = lax.axis_index("tile")
    rows = per_dev * rank_most
    for d in range(tile_count):
        place = pl.multiple_of((me ^ d) * rows, rows)
        for b in range(inner):
            held[b, pl.ds(place, rows)] = in_refs[d][b].reshape(rows, 2 * sources)
    for b in range(inner):
        span = slice(b * width, (b + 1) * width)
        turned = held[b].T
        by_real = jnp.dot(
            turned,
            factors_ref[:, 0, :, span].reshape(outer * rank_most, width),
            preferred_element_type=F32,
        )
        by_imag = jnp.dot(
            turned,
            factors_ref[:, 1, :, span].reshape(outer * rank_most, width),
            preferred_element_type=F32,
        )
        if conjugate:
            real = by_real[:sources] + by_imag[sources:]
            imag = by_real[sources:] - by_imag[:sources]
        else:
            real = by_real[:sources] - by_imag[sources:]
            imag = by_real[sources:] + by_imag[:sources]
        out_ref[0, :, span] = real.astype(BF16)
        out_ref[1, :, span] = imag.astype(BF16)
    if split > 1:
        group = lax.axis_index("freq")
        share = sources // split
        for d in range(split):
            place = pl.multiple_of((group ^ d) * share, share)
            split_refs[d][...] = out_ref[:, pl.ds(place, share)]


def gate_kernel(freqs, gate_ref, *refs):
    in_refs, out_refs = refs[:freqs], refs[freqs:]
    group = lax.axis_index("freq")
    parts = [(ref[0].astype(F32), ref[1].astype(F32)) for ref in in_refs]
    for d in range(freqs):
        target = group ^ d
        real = imag = None
        for e, (x, y) in enumerate(parts):
            g = gate_ref[0, target, group ^ e]
            h = gate_ref[1, target, group ^ e]
            first = g * x - h * y
            second = g * y + h * x
            real = first if real is None else real + first
            imag = second if imag is None else imag + second
        out_refs[d][0] = real.astype(BF16)
        out_refs[d][1] = imag.astype(BF16)


def call(kernel, out_shape, specs, scratch, args, flops):
    held = sum(a.size * a.dtype.itemsize for a in args)
    held += sum(o.size * o.dtype.itemsize for o in out_shape)
    return pl.pallas_call(
        kernel,
        out_shape=out_shape,
        in_specs=specs,
        out_specs=[VMEM] * len(out_shape),
        scratch_shapes=scratch,
        compiler_params=pltpu.CompilerParams(vmem_limit_bytes=2 * held + (8 << 20)),
        cost_estimate=pl.CostEstimate(flops=flops, bytes_accessed=held, transcendentals=0),
    )(*args)


def shards(signal, v_factors, u_factors, tile_ranks, row_order, col_order, time_gate):
    tile_count = lax.axis_size("tile")
    freqs = lax.axis_size("freq")
    row_tiles, _, rank_most, col_local = v_factors.shape[1:]
    col_tiles = u_factors.shape[1]
    row_local = u_factors.shape[4]
    sources = signal.shape[2]
    col_dev = col_tiles // tile_count
    row_dev = row_tiles // tile_count
    width = col_local // col_dev
    share = sources // freqs
    flops = 8 * row_tiles * col_dev * rank_most * width * sources
    right, left = v_factors[0], u_factors[0]
    ranks = tile_ranks[0]
    tile_order = partner_order(tile_count)
    freq_order = list(range(freqs - 1, 0, -1))

    def analysis(factors, spectra, outer, inner, conjugate):
        per_dev = outer // tile_count
        dims = (tile_count, outer, inner, rank_most, width, sources, conjugate)
        block = jax.ShapeDtypeStruct((per_dev, inner, rank_most, 2 * sources), BF16)
        return call(
            functools.partial(analysis_kernel, dims),
            [block] * tile_count,
            [SMEM] * 3 + [VMEM] * (1 + len(spectra)),
            [
                pltpu.VMEM((2, 2, sources, inner * width), BF16),
                pltpu.VMEM((outer, inner, rank_most, 2 * sources), BF16),
            ],
            (ranks, row_order, col_order, factors, *spectra),
            flops,
        )

    def synthesis(factors, blocks, outer, inner, conjugate, split):
        dims = (tile_count, outer, inner, rank_most, width, sources, conjugate, split)
        shapes = [jax.ShapeDtypeStruct((2, sources, inner * width), BF16)]
        if split > 1:
            shapes += [jax.ShapeDtypeStruct((2, sources // split, inner * width), BF16)] * split
        return call(
            functools.partial(synthesis_kernel, dims),
            shapes,
            [VMEM] * (1 + tile_count),
            [pltpu.VMEM((inner, outer * rank_most, 2 * sources), BF16)],
            (factors, *blocks),
            flops,
        )

    sent = analysis(right, (signal[0],), row_tiles, col_dev, False)
    got = exchange(sent, "tile", tile_order)
    forward, *pieces = synthesis(left, got, col_tiles, row_dev, False, freqs)
    pieces = exchange(pieces, "freq", freq_order)
    gated = call(
        functools.partial(gate_kernel, freqs),
        [jax.ShapeDtypeStruct((2, share, row_local), BF16)] * freqs,
        [SMEM] + [VMEM] * freqs,
        [],
        (time_gate, *pieces),
        16 * freqs * freqs * share * row_local,
    )
    gated = exchange(gated, "freq", freq_order)
    sent = analysis(left, tuple(gated), col_tiles, row_dev, True)
    got = exchange(sent, "tile", tile_order)
    (adjoint,) = synthesis(right, got, row_tiles, col_dev, True, 1)
    return forward[None], adjoint[None]


def solution(mesh):
    return jax.shard_map(
        shards,
        mesh=mesh,
        in_specs=(
            P("freq", None, None, "tile"),
            P("freq", None, None, None, "tile"),
            P("freq", None, None, None, "tile"),
            P("freq", None, None),
            P(),
            P(),
            P(),
        ),
        out_specs=(P("freq", None, None, "tile"), P("freq", None, None, "tile")),
        check_vma=False,
    )
```

```python
import functools

import jax
import jax.numpy as jnp
from jax import lax
from jax.experimental import pallas as pl
from jax.experimental.pallas import tpu as pltpu
from jax.sharding import PartitionSpec as P


F32 = jnp.float32
BF16 = jnp.bfloat16
VMEM = pl.BlockSpec(memory_space=pltpu.VMEM)
SMEM = pl.BlockSpec(memory_space=pltpu.SMEM)
HBM = pl.BlockSpec(memory_space=pltpu.HBM)
NT = (((1,), (1,)), ((), ()))


def tile_order(count):
    chips = sorted(range(1, count // 2), key=lambda g: (bin(g).count("1"), g))
    return [2 * g + c for g in chips for c in (0, 1)] + [1, 0]


def freq_order(count):
    return list(range(count - 1, -1, -1))


def exchange(blocks, axis, order):
    pairs = {d: [(i, i ^ d) for i in range(len(order))] for d in order}
    return [lax.ppermute(x, axis, pairs[d]) if d else x for x, d in zip(blocks, order)]


def analysis_kernel(dims, *refs):
    tile_count, outer, inner, rank_most, width, sources, conjugate, pieces = dims
    ranks_ref, rows_ref, cols_ref, factors_ref = refs[:4]
    spectra_refs = refs[4 : 4 + pieces]
    out_refs = refs[4 + pieces : 4 + pieces + tile_count]
    weights, *fetched = refs[4 + pieces + tile_count :]
    per_dev = outer // tile_count
    order = tile_order(tile_count)
    me = lax.axis_index("tile")
    chips = [d // 2 for d in order[::2]]
    firsts = [((me // 2) ^ g) * 2 * per_dev for g in chips]

    if fetched:
        *tables, held, spectrum, sems = fetched
        moves = [(spectra_refs[0], spectrum), *zip((ranks_ref, rows_ref, cols_ref), tables)]
        for n, first in enumerate(firsts):
            place = pl.ds(n * 2 * per_dev, 2 * per_dev)
            moves.append((factors_ref.at[pl.ds(first, 2 * per_dev)], held.at[place]))
        copies = [pltpu.make_async_copy(x, y, sems.at[i]) for i, (x, y) in enumerate(moves)]
        for copy in copies:
            copy.start()
        for copy in copies[:4]:
            copy.wait()
        ranks_ref, rows_ref, cols_ref = tables
        spectra = [(slice(None), spectrum[0], spectrum[1])]
    else:
        share = sources // pieces
        here = lax.axis_index("freq")
        spectra = [
            (pl.ds(pl.multiple_of((here ^ d) * share, share), share), ref[0], ref[1])
            for ref, d in zip(spectra_refs, freq_order(pieces))
        ]
    for where, real, imag in spectra:
        weights[0, 0, where] = real
        weights[0, 1, where] = imag
        weights[1, 0, where] = imag if conjugate else -imag
        weights[1, 1, where] = -real if conjugate else real
    slots = lax.broadcasted_iota(jnp.int32, (rank_most, 2 * sources), 0)
    for n, (g, first) in enumerate(zip(chips, firsts)):
        offsets = [((me & 1) ^ c) * per_dev for c in (0, 1)]
        source, base = factors_ref, first
        if fetched:
            copies[4 + n].wait()
            source, base = held, n * 2 * per_dev
        for b in range(inner):
            span = slice(b * width, (b + 1) * width)
            here = me * inner + b
            total = None
            for p in range(2):
                factor = jnp.concatenate(
                    [
                        source[pl.ds(base + o, per_dev), p, :, span].reshape(-1, width)
                        for o in offsets
                    ]
                )
                weight = weights[p, :, :, span].reshape(2 * sources, width)
                term = lax.dot_general(factor, weight, NT, preferred_element_type=F32)
                total = term if total is None else total + term
            for c in (0, 1):
                for a in range(per_dev):
                    there = first + offsets[c] + a
                    row, col = (here, there) if conjugate else (there, here)
                    live = ranks_ref[rows_ref[row], cols_ref[col]]
                    at = (c * per_dev + a) * rank_most
                    part = jnp.where(slots < live, total[at : at + rank_most], 0.0)
                    out_refs[order.index(2 * g + c)][a, b] = part.astype(BF16)


def synthesis_kernel(dims, factors_ref, *refs):
    tile_count, outer, inner, rank_most, width, sources, conjugate, split = dims
    per_dev = outer // tile_count
    in_refs = refs[:tile_count]
    out_ref = refs[tile_count]
    split_refs = refs[tile_count + 1 : -1]
    held = refs[-1]
    me = lax.axis_index("tile")
    rows = per_dev * rank_most
    for ref, d in zip(in_refs, tile_order(tile_count)):
        place = pl.multiple_of((me ^ d) * rows, rows)
        for b in range(inner):
            held[b, pl.ds(place, rows)] = ref[b].reshape(rows, 2 * sources)
    for b in range(inner):
        span = slice(b * width, (b + 1) * width)
        turned = held[b].T
        by_real = jnp.dot(
            turned,
            factors_ref[:, 0, :, span].reshape(outer * rank_most, width),
            preferred_element_type=F32,
        )
        by_imag = jnp.dot(
            turned,
            factors_ref[:, 1, :, span].reshape(outer * rank_most, width),
            preferred_element_type=F32,
        )
        if conjugate:
            real = by_real[:sources] + by_imag[sources:]
            imag = by_real[sources:] - by_imag[:sources]
        else:
            real = by_real[:sources] - by_imag[sources:]
            imag = by_real[sources:] + by_imag[:sources]
        out_ref[0, :, span] = real.astype(BF16)
        out_ref[1, :, span] = imag.astype(BF16)
    if split > 1:
        group = lax.axis_index("freq")
        share = sources // split
        for ref, d in zip(split_refs, freq_order(split)):
            place = pl.multiple_of((group ^ d) * share, share)
            ref[...] = out_ref[:, pl.ds(place, share)]


def gate_kernel(freqs, gate_ref, *refs):
    in_refs, out_refs = refs[:freqs], refs[freqs:]
    group = lax.axis_index("freq")
    parts = [(ref[0].astype(F32), ref[1].astype(F32)) for ref in in_refs]
    order = freq_order(freqs)
    for ref, d in zip(out_refs, order):
        target = group ^ d
        real = imag = None
        for (x, y), e in zip(parts, order):
            g = gate_ref[0, target, group ^ e]
            h = gate_ref[1, target, group ^ e]
            first = g * x - h * y
            second = g * y + h * x
            real = first if real is None else real + first
            imag = second if imag is None else imag + second
        ref[0] = real.astype(BF16)
        ref[1] = imag.astype(BF16)


def call(kernel, out_shape, specs, scratch, args, flops):
    held = sum(a.size * a.dtype.itemsize for a in args)
    held += sum(o.size * o.dtype.itemsize for o in out_shape)
    return pl.pallas_call(
        kernel,
        out_shape=out_shape,
        in_specs=specs,
        out_specs=[VMEM] * len(out_shape),
        scratch_shapes=scratch,
        compiler_params=pltpu.CompilerParams(vmem_limit_bytes=2 * held + (8 << 20)),
        cost_estimate=pl.CostEstimate(flops=flops, bytes_accessed=held, transcendentals=0),
    )(*args)


def shards(signal, v_factors, u_factors, tile_ranks, row_order, col_order, time_gate):
    tile_count = lax.axis_size("tile")
    freqs = lax.axis_size("freq")
    row_tiles, _, rank_most, col_local = v_factors.shape[1:]
    col_tiles = u_factors.shape[1]
    row_local = u_factors.shape[4]
    sources = signal.shape[2]
    col_dev = col_tiles // tile_count
    row_dev = row_tiles // tile_count
    width = col_local // col_dev
    share = sources // freqs
    flops = 8 * row_tiles * col_dev * rank_most * width * sources
    right, left = v_factors[0], u_factors[0]
    ranks = tile_ranks[0]

    def analysis(factors, spectra, outer, inner, conjugate, fetch):
        per_dev = outer // tile_count
        pieces = len(spectra)
        dims = (tile_count, outer, inner, rank_most, width, sources, conjugate, pieces)
        block = jax.ShapeDtypeStruct((per_dev, inner, rank_most, 2 * sources), BF16)
        tables = (ranks, row_order, col_order)
        specs = [SMEM] * 3 + [VMEM] * (1 + pieces)
        scratch = [pltpu.VMEM((2, 2, sources, inner * width), BF16)]
        if fetch:
            specs = [HBM] * (4 + pieces)
            scratch += [pltpu.SMEM(x.shape, x.dtype) for x in tables]
            scratch += [pltpu.VMEM(x.shape, x.dtype) for x in (factors, *spectra)]
            scratch += [pltpu.SemaphoreType.DMA((4 + tile_count // 2,))]
        return call(
            functools.partial(analysis_kernel, dims),
            [block] * tile_count,
            specs,
            scratch,
            (*tables, factors, *spectra),
            flops,
        )

    def synthesis(factors, blocks, outer, inner, conjugate, split):
        dims = (tile_count, outer, inner, rank_most, width, sources, conjugate, split)
        shapes = [jax.ShapeDtypeStruct((2, sources, inner * width), BF16)]
        if split > 1:
            shapes += [jax.ShapeDtypeStruct((2, sources // split, inner * width), BF16)] * split
        return call(
            functools.partial(synthesis_kernel, dims),
            shapes,
            [VMEM] * (1 + tile_count),
            [pltpu.VMEM((inner, outer * rank_most, 2 * sources), BF16)],
            (factors, *blocks),
            flops,
        )

    sent = analysis(right, (signal[0],), row_tiles, col_dev, False, True)
    got = exchange(sent, "tile", tile_order(tile_count))
    forward, *pieces = synthesis(left, got, col_tiles, row_dev, False, freqs)
    pieces = exchange(pieces, "freq", freq_order(freqs))
    gated = call(
        functools.partial(gate_kernel, freqs),
        [jax.ShapeDtypeStruct((2, share, row_local), BF16)] * freqs,
        [SMEM] + [VMEM] * freqs,
        [],
        (time_gate, *pieces),
        16 * freqs * freqs * share * row_local,
    )
    gated = exchange(gated, "freq", freq_order(freqs))
    sent = analysis(left, tuple(gated), col_tiles, row_dev, True, False)
    got = exchange(sent, "tile", tile_order(tile_count))
    (adjoint,) = synthesis(right, got, row_tiles, col_dev, True, 1)
    return forward[None], adjoint[None]


def solution(mesh):
    return jax.shard_map(
        shards,
        mesh=mesh,
        in_specs=(
            P("freq", None, None, "tile"),
            P("freq", None, None, None, "tile"),
            P("freq", None, None, None, "tile"),
            P("freq", None, None),
            P(),
            P(),
            P(),
        ),
        out_specs=(P("freq", None, None, "tile"), P("freq", None, None, "tile")),
        check_vma=False,
    )
```

```python
import functools

import jax
import jax.numpy as jnp
from jax import lax
from jax.experimental import pallas as pl
from jax.experimental.pallas import tpu as pltpu
from jax.sharding import PartitionSpec as P


F32 = jnp.float32
BF16 = jnp.bfloat16
VMEM = pl.BlockSpec(memory_space=pltpu.VMEM)
SMEM = pl.BlockSpec(memory_space=pltpu.SMEM)
HBM = pl.BlockSpec(memory_space=pltpu.HBM)
NT = (((1,), (1,)), ((), ()))


def tile_order(count):
    chips = sorted(range(1, count // 2), key=lambda g: (bin(g).count("1"), g))
    return [2 * g + c for g in chips for c in (0, 1)] + [1, 0]


def freq_order(count):
    return list(range(count - 1, -1, -1))


def exchange(blocks, axis, order):
    pairs = {d: [(i, i ^ d) for i in range(len(order))] for d in order}
    return [lax.ppermute(x, axis, pairs[d]) if d else x for x, d in zip(blocks, order)]


def analysis_kernel(dims, *refs):
    tile_count, outer, inner, rank_most, width, sources, conjugate, pieces = dims
    ranks_ref, rows_ref, cols_ref, factors_ref = refs[:4]
    spectra_refs = refs[4 : 4 + pieces]
    out_refs = refs[4 + pieces : 4 + pieces + tile_count]
    weights, *fetched = refs[4 + pieces + tile_count :]
    per_dev = outer // tile_count
    order = tile_order(tile_count)
    me = lax.axis_index("tile")
    chips = [d // 2 for d in order[::2]]
    firsts = [((me // 2) ^ g) * 2 * per_dev for g in chips]

    if fetched:
        *tables, held, spectrum, sems = fetched
        moves = [(spectra_refs[0], spectrum), *zip((ranks_ref, rows_ref, cols_ref), tables)]
        for n, first in enumerate(firsts):
            place = pl.ds(n * 2 * per_dev, 2 * per_dev)
            moves.append((factors_ref.at[pl.ds(first, 2 * per_dev)], held.at[place]))
        copies = [pltpu.make_async_copy(x, y, sems.at[i]) for i, (x, y) in enumerate(moves)]
        for copy in copies:
            copy.start()
        for copy in copies[:4]:
            copy.wait()
        ranks_ref, rows_ref, cols_ref = tables
        spectra = [(slice(None), spectrum[0], spectrum[1])]
    else:
        share = sources // pieces
        here = lax.axis_index("freq")
        spectra = [
            (pl.ds(pl.multiple_of((here ^ d) * share, share), share), ref[0], ref[1])
            for ref, d in zip(spectra_refs, freq_order(pieces))
        ]
    for where, real, imag in spectra:
        weights[0, 0, where] = real
        weights[0, 1, where] = imag
        weights[1, 0, where] = imag if conjugate else -imag
        weights[1, 1, where] = -real if conjugate else real
    slots = lax.broadcasted_iota(jnp.int32, (rank_most, 2 * sources), 0)
    for n, (g, first) in enumerate(zip(chips, firsts)):
        offsets = [((me & 1) ^ c) * per_dev for c in (0, 1)]
        source, base = factors_ref, first
        if fetched:
            copies[4 + n].wait()
            source, base = held, n * 2 * per_dev
        for b in range(inner):
            span = slice(b * width, (b + 1) * width)
            here = me * inner + b
            total = None
            for p in range(2):
                factor = jnp.concatenate(
                    [
                        source[pl.ds(base + o, per_dev), p, :, span].reshape(-1, width)
                        for o in offsets
                    ]
                )
                weight = weights[p, :, :, span].reshape(2 * sources, width)
                term = lax.dot_general(factor, weight, NT, preferred_element_type=F32)
                total = term if total is None else total + term
            for c in (0, 1):
                for a in range(per_dev):
                    there = first + offsets[c] + a
                    row, col = (here, there) if conjugate else (there, here)
                    live = ranks_ref[rows_ref[row], cols_ref[col]]
                    at = (c * per_dev + a) * rank_most
                    part = jnp.where(slots < live, total[at : at + rank_most], 0.0)
                    out_refs[order.index(2 * g + c)][a, b] = part.astype(BF16)


def synthesis_kernel(dims, factors_ref, *refs):
    tile_count, outer, inner, rank_most, width, sources, conjugate, split = dims
    per_dev = outer // tile_count
    in_refs = refs[:tile_count]
    out_ref = refs[tile_count]
    split_refs = refs[tile_count + 1 : -1]
    held = refs[-1]
    me = lax.axis_index("tile")
    rows = per_dev * rank_most
    for ref, d in zip(in_refs, tile_order(tile_count)):
        place = pl.multiple_of((me ^ d) * rows, rows)
        for b in range(inner):
            held[b, pl.ds(place, rows)] = ref[b].reshape(rows, 2 * sources)
    for b in range(inner):
        span = slice(b * width, (b + 1) * width)
        turned = held[b].T
        by_real = jnp.dot(
            turned,
            factors_ref[:, 0, :, span].reshape(outer * rank_most, width),
            preferred_element_type=F32,
        )
        by_imag = jnp.dot(
            turned,
            factors_ref[:, 1, :, span].reshape(outer * rank_most, width),
            preferred_element_type=F32,
        )
        if conjugate:
            real = by_real[:sources] + by_imag[sources:]
            imag = by_real[sources:] - by_imag[:sources]
        else:
            real = by_real[:sources] - by_imag[sources:]
            imag = by_real[sources:] + by_imag[:sources]
        out_ref[0, :, span] = real.astype(BF16)
        out_ref[1, :, span] = imag.astype(BF16)
    if split > 1:
        group = lax.axis_index("freq")
        share = sources // split
        for ref, d in zip(split_refs, freq_order(split)):
            place = pl.multiple_of((group ^ d) * share, share)
            ref[...] = out_ref[:, pl.ds(place, share)]


def gate_kernel(freqs, gate_ref, *refs):
    in_refs, out_refs = refs[:freqs], refs[freqs:]
    group = lax.axis_index("freq")
    parts = [(ref[0].astype(F32), ref[1].astype(F32)) for ref in in_refs]
    order = freq_order(freqs)
    for ref, d in zip(out_refs, order):
        target = group ^ d
        real = imag = None
        for (x, y), e in zip(parts, order):
            g = gate_ref[0, target, group ^ e]
            h = gate_ref[1, target, group ^ e]
            first = g * x - h * y
            second = g * y + h * x
            real = first if real is None else real + first
            imag = second if imag is None else imag + second
        ref[0] = real.astype(BF16)
        ref[1] = imag.astype(BF16)


def call(kernel, out_shape, specs, scratch, args, flops):
    held = sum(a.size * a.dtype.itemsize for a in args)
    held += sum(o.size * o.dtype.itemsize for o in out_shape)
    return pl.pallas_call(
        kernel,
        out_shape=out_shape,
        in_specs=specs,
        out_specs=[VMEM] * len(out_shape),
        scratch_shapes=scratch,
        compiler_params=pltpu.CompilerParams(vmem_limit_bytes=2 * held + (8 << 20)),
        cost_estimate=pl.CostEstimate(flops=flops, bytes_accessed=held, transcendentals=0),
    )(*args)


def shards(signal, v_factors, u_factors, tile_ranks, row_order, col_order, time_gate):
    tile_count = lax.axis_size("tile")
    freqs = lax.axis_size("freq")
    row_tiles, _, rank_most, col_local = v_factors.shape[1:]
    col_tiles = u_factors.shape[1]
    row_local = u_factors.shape[4]
    sources = signal.shape[2]
    col_dev = col_tiles // tile_count
    row_dev = row_tiles // tile_count
    width = col_local // col_dev
    share = sources // freqs
    flops = 8 * row_tiles * col_dev * rank_most * width * sources
    right, left = v_factors[0], u_factors[0]
    ranks = tile_ranks[0]

    def analysis(factors, spectra, outer, inner, conjugate, fetch):
        per_dev = outer // tile_count
        pieces = len(spectra)
        dims = (tile_count, outer, inner, rank_most, width, sources, conjugate, pieces)
        block = jax.ShapeDtypeStruct((per_dev, inner, rank_most, 2 * sources), BF16)
        tables = (ranks, row_order, col_order)
        specs = [SMEM] * 3 + [VMEM] * (1 + pieces)
        scratch = [pltpu.VMEM((2, 2, sources, inner * width), BF16)]
        if fetch:
            specs = [HBM] * (4 + pieces)
            scratch += [pltpu.SMEM(x.shape, x.dtype) for x in tables]
            scratch += [pltpu.VMEM(x.shape, x.dtype) for x in (factors, *spectra)]
            scratch += [pltpu.SemaphoreType.DMA((4 + tile_count // 2,))]
            tables = tuple(pltpu.with_memory_space_constraint(x, pltpu.HBM) for x in tables)
            factors = pltpu.with_memory_space_constraint(factors, pltpu.HBM)
            spectra = tuple(pltpu.with_memory_space_constraint(x, pltpu.HBM) for x in spectra)
        return call(
            functools.partial(analysis_kernel, dims),
            [block] * tile_count,
            specs,
            scratch,
            (*tables, factors, *spectra),
            flops,
        )

    def synthesis(factors, blocks, outer, inner, conjugate, split):
        dims = (tile_count, outer, inner, rank_most, width, sources, conjugate, split)
        shapes = [jax.ShapeDtypeStruct((2, sources, inner * width), BF16)]
        if split > 1:
            shapes += [jax.ShapeDtypeStruct((2, sources // split, inner * width), BF16)] * split
        return call(
            functools.partial(synthesis_kernel, dims),
            shapes,
            [VMEM] * (1 + tile_count),
            [pltpu.VMEM((inner, outer * rank_most, 2 * sources), BF16)],
            (factors, *blocks),
            flops,
        )

    sent = analysis(right, (signal[0],), row_tiles, col_dev, False, True)
    got = exchange(sent, "tile", tile_order(tile_count))
    forward, *pieces = synthesis(left, got, col_tiles, row_dev, False, freqs)
    pieces = exchange(pieces, "freq", freq_order(freqs))
    gated = call(
        functools.partial(gate_kernel, freqs),
        [jax.ShapeDtypeStruct((2, share, row_local), BF16)] * freqs,
        [SMEM] + [VMEM] * freqs,
        [],
        (time_gate, *pieces),
        16 * freqs * freqs * share * row_local,
    )
    gated = exchange(gated, "freq", freq_order(freqs))
    sent = analysis(left, tuple(gated), col_tiles, row_dev, True, False)
    got = exchange(sent, "tile", tile_order(tile_count))
    (adjoint,) = synthesis(right, got, row_tiles, col_dev, True, 1)
    return forward[None], adjoint[None]


def solution(mesh):
    return jax.shard_map(
        shards,
        mesh=mesh,
        in_specs=(
            P("freq", None, None, "tile"),
            P("freq", None, None, None, "tile"),
            P("freq", None, None, None, "tile"),
            P("freq", None, None),
            P(),
            P(),
            P(),
        ),
        out_specs=(P("freq", None, None, "tile"), P("freq", None, None, "tile")),
        check_vma=False,
    )
```

```python
import functools

import jax
import jax.numpy as jnp
from jax import lax
from jax.experimental import pallas as pl
from jax.experimental.pallas import tpu as pltpu
from jax.sharding import PartitionSpec as P


F32 = jnp.float32
BF16 = jnp.bfloat16
VMEM = pl.BlockSpec(memory_space=pltpu.VMEM)
SMEM = pl.BlockSpec(memory_space=pltpu.SMEM)
HBM = pl.BlockSpec(memory_space=pltpu.HBM)
NT = (((1,), (1,)), ((), ()))


def tile_plan(count):
    first = sorted(range(1, count // 2), key=lambda g: (bin(g).count("1"), g))
    second = list(first)
    for n in range(0, len(first) - 1, 2):
        second[n], second[n + 1] = first[n + 1], first[n]
    chips = list(zip(first, second))
    return [(2 * g + c, 2 * h + c) for c in (0, 1) for g, h in chips] + [(1, 1), (0, 0)]


def freq_plan(count):
    return [(d, d) for d in range(count - 1, -1, -1)]


def pick(pair, core):
    return pair[0] + core * (pair[1] - pair[0])


def came_from(step, core):
    return pick(step if step[0] % 2 == 0 else step[::-1], core)


def exchange(blocks, axis, plan):
    count = len(plan)
    return [
        lax.ppermute(x, axis, [(i, i ^ step[i % 2]) for i in range(count)]) if step[0] else x
        for x, step in zip(blocks, plan)
    ]


def analysis_kernel(dims, *refs):
    tile_count, outer, inner, rank_most, width, sources, conjugate, pieces = dims
    ranks_ref, rows_ref, cols_ref, factors_ref = refs[:4]
    spectra_refs = refs[4 : 4 + pieces]
    out_refs = refs[4 + pieces : 4 + pieces + tile_count]
    weights, *fetched = refs[4 + pieces + tile_count :]
    per_dev = outer // tile_count
    me = lax.axis_index("tile")
    core = me % 2
    plan = tile_plan(tile_count)
    half = tile_count // 2
    chips = [(step, n, half - 1 + n) for n, step in enumerate(plan[: half - 1])]
    chips.append((plan[-1], tile_count - 1, tile_count - 2))
    firsts = [((me ^ pick(step, core)) // 2) * 2 * per_dev for step, _, _ in chips]

    if fetched:
        *tables, held, spectrum, sems = fetched
        moves = [(spectra_refs[0], spectrum), *zip((ranks_ref, rows_ref, cols_ref), tables)]
        for n, first in enumerate(firsts):
            place = pl.ds(n * 2 * per_dev, 2 * per_dev)
            moves.append((factors_ref.at[pl.ds(first, 2 * per_dev)], held.at[place]))
        copies = [pltpu.make_async_copy(x, y, sems.at[i]) for i, (x, y) in enumerate(moves)]
        for copy in copies:
            copy.start()
        for copy in copies[:4]:
            copy.wait()
        ranks_ref, rows_ref, cols_ref = tables
        spectra = [(slice(None), spectrum[0], spectrum[1])]
    else:
        share = sources // pieces
        here = lax.axis_index("freq")
        spectra = [
            (pl.ds(pl.multiple_of((here ^ step[0]) * share, share), share), ref[0], ref[1])
            for ref, step in zip(spectra_refs, freq_plan(pieces))
        ]
    for where, real, imag in spectra:
        weights[0, 0, where] = real
        weights[0, 1, where] = imag
        weights[1, 0, where] = imag if conjugate else -imag
        weights[1, 1, where] = -real if conjugate else real
    slots = lax.broadcasted_iota(jnp.int32, (rank_most, 2 * sources), 0)
    offsets = [core * per_dev, (1 - core) * per_dev]
    for n, ((_, *steps), first) in enumerate(zip(chips, firsts)):
        source, base = factors_ref, first
        if fetched:
            copies[4 + n].wait()
            source, base = held, n * 2 * per_dev
        for b in range(inner):
            span = slice(b * width, (b + 1) * width)
            here = me * inner + b
            total = None
            for p in range(2):
                factor = jnp.concatenate(
                    [
                        source[pl.ds(base + o, per_dev), p, :, span].reshape(-1, width)
                        for o in offsets
                    ]
                )
                weight = weights[p, :, :, span].reshape(2 * sources, width)
                term = lax.dot_general(factor, weight, NT, preferred_element_type=F32)
                total = term if total is None else total + term
            for c in (0, 1):
                for a in range(per_dev):
                    there = first + offsets[c] + a
                    row, col = (here, there) if conjugate else (there, here)
                    live = ranks_ref[rows_ref[row], cols_ref[col]]
                    at = (c * per_dev + a) * rank_most
                    part = jnp.where(slots < live, total[at : at + rank_most], 0.0)
                    out_refs[steps[c]][a, b] = part.astype(BF16)


def synthesis_kernel(dims, factors_ref, *refs):
    tile_count, outer, inner, rank_most, width, sources, conjugate, split = dims
    per_dev = outer // tile_count
    in_refs = refs[:tile_count]
    out_ref = refs[tile_count]
    split_refs = refs[tile_count + 1 : -1]
    held = refs[-1]
    me = lax.axis_index("tile")
    rows = per_dev * rank_most
    for ref, step in zip(in_refs, tile_plan(tile_count)):
        place = pl.multiple_of((me ^ came_from(step, me % 2)) * rows, rows)
        for b in range(inner):
            held[b, pl.ds(place, rows)] = ref[b].reshape(rows, 2 * sources)
    for b in range(inner):
        span = slice(b * width, (b + 1) * width)
        turned = held[b].T
        by_real = jnp.dot(
            turned,
            factors_ref[:, 0, :, span].reshape(outer * rank_most, width),
            preferred_element_type=F32,
        )
        by_imag = jnp.dot(
            turned,
            factors_ref[:, 1, :, span].reshape(outer * rank_most, width),
            preferred_element_type=F32,
        )
        if conjugate:
            real = by_real[:sources] + by_imag[sources:]
            imag = by_real[sources:] - by_imag[:sources]
        else:
            real = by_real[:sources] - by_imag[sources:]
            imag = by_real[sources:] + by_imag[:sources]
        out_ref[0, :, span] = real.astype(BF16)
        out_ref[1, :, span] = imag.astype(BF16)
    if split > 1:
        group = lax.axis_index("freq")
        share = sources // split
        for ref, step in zip(split_refs, freq_plan(split)):
            place = pl.multiple_of((group ^ step[0]) * share, share)
            ref[...] = out_ref[:, pl.ds(place, share)]


def gate_kernel(freqs, gate_ref, *refs):
    in_refs, out_refs = refs[:freqs], refs[freqs:]
    group = lax.axis_index("freq")
    parts = [(ref[0].astype(F32), ref[1].astype(F32)) for ref in in_refs]
    order = [step[0] for step in freq_plan(freqs)]
    for ref, d in zip(out_refs, order):
        target = group ^ d
        real = imag = None
        for (x, y), e in zip(parts, order):
            g = gate_ref[0, target, group ^ e]
            h = gate_ref[1, target, group ^ e]
            first = g * x - h * y
            second = g * y + h * x
            real = first if real is None else real + first
            imag = second if imag is None else imag + second
        ref[0] = real.astype(BF16)
        ref[1] = imag.astype(BF16)


def call(kernel, out_shape, specs, scratch, args, flops):
    held = sum(a.size * a.dtype.itemsize for a in args)
    held += sum(o.size * o.dtype.itemsize for o in out_shape)
    return pl.pallas_call(
        kernel,
        out_shape=out_shape,
        in_specs=specs,
        out_specs=[VMEM] * len(out_shape),
        scratch_shapes=scratch,
        compiler_params=pltpu.CompilerParams(vmem_limit_bytes=2 * held + (8 << 20)),
        cost_estimate=pl.CostEstimate(flops=flops, bytes_accessed=held, transcendentals=0),
    )(*args)


def shards(signal, v_factors, u_factors, tile_ranks, row_order, col_order, time_gate):
    tile_count = lax.axis_size("tile")
    freqs = lax.axis_size("freq")
    row_tiles, _, rank_most, col_local = v_factors.shape[1:]
    col_tiles = u_factors.shape[1]
    row_local = u_factors.shape[4]
    sources = signal.shape[2]
    col_dev = col_tiles // tile_count
    row_dev = row_tiles // tile_count
    width = col_local // col_dev
    share = sources // freqs
    flops = 8 * row_tiles * col_dev * rank_most * width * sources
    right, left = v_factors[0], u_factors[0]
    ranks = tile_ranks[0]

    def analysis(factors, spectra, outer, inner, conjugate, fetch):
        per_dev = outer // tile_count
        pieces = len(spectra)
        dims = (tile_count, outer, inner, rank_most, width, sources, conjugate, pieces)
        block = jax.ShapeDtypeStruct((per_dev, inner, rank_most, 2 * sources), BF16)
        tables = (ranks, row_order, col_order)
        specs = [SMEM] * 3 + [VMEM] * (1 + pieces)
        scratch = [pltpu.VMEM((2, 2, sources, inner * width), BF16)]
        if fetch:
            specs = [HBM] * (4 + pieces)
            scratch += [pltpu.SMEM(x.shape, x.dtype) for x in tables]
            scratch += [pltpu.VMEM(x.shape, x.dtype) for x in (factors, *spectra)]
            scratch += [pltpu.SemaphoreType.DMA((4 + tile_count // 2,))]
            tables = tuple(pltpu.with_memory_space_constraint(x, pltpu.HBM) for x in tables)
            factors = pltpu.with_memory_space_constraint(factors, pltpu.HBM)
            spectra = tuple(pltpu.with_memory_space_constraint(x, pltpu.HBM) for x in spectra)
        return call(
            functools.partial(analysis_kernel, dims),
            [block] * tile_count,
            specs,
            scratch,
            (*tables, factors, *spectra),
            flops,
        )

    def synthesis(factors, blocks, outer, inner, conjugate, split):
        dims = (tile_count, outer, inner, rank_most, width, sources, conjugate, split)
        shapes = [jax.ShapeDtypeStruct((2, sources, inner * width), BF16)]
        if split > 1:
            shapes += [jax.ShapeDtypeStruct((2, sources // split, inner * width), BF16)] * split
        return call(
            functools.partial(synthesis_kernel, dims),
            shapes,
            [VMEM] * (1 + tile_count),
            [pltpu.VMEM((inner, outer * rank_most, 2 * sources), BF16)],
            (factors, *blocks),
            flops,
        )

    sent = analysis(right, (signal[0],), row_tiles, col_dev, False, True)
    got = exchange(sent, "tile", tile_plan(tile_count))
    forward, *pieces = synthesis(left, got, col_tiles, row_dev, False, freqs)
    pieces = exchange(pieces, "freq", freq_plan(freqs))
    gated = call(
        functools.partial(gate_kernel, freqs),
        [jax.ShapeDtypeStruct((2, share, row_local), BF16)] * freqs,
        [SMEM] + [VMEM] * freqs,
        [],
        (time_gate, *pieces),
        16 * freqs * freqs * share * row_local,
    )
    gated = exchange(gated, "freq", freq_plan(freqs))
    sent = analysis(left, tuple(gated), col_tiles, row_dev, True, False)
    got = exchange(sent, "tile", tile_plan(tile_count))
    (adjoint,) = synthesis(right, got, row_tiles, col_dev, True, 1)
    return forward[None], adjoint[None]


def solution(mesh):
    return jax.shard_map(
        shards,
        mesh=mesh,
        in_specs=(
            P("freq", None, None, "tile"),
            P("freq", None, None, None, "tile"),
            P("freq", None, None, None, "tile"),
            P("freq", None, None),
            P(),
            P(),
            P(),
        ),
        out_specs=(P("freq", None, None, "tile"), P("freq", None, None, "tile")),
        check_vma=False,
    )
```

```python
import functools

import jax
import jax.numpy as jnp
from jax import lax
from jax.experimental import pallas as pl
from jax.experimental.pallas import tpu as pltpu
from jax.sharding import PartitionSpec as P


F32 = jnp.float32
BF16 = jnp.bfloat16
VMEM = pl.BlockSpec(memory_space=pltpu.VMEM)
SMEM = pl.BlockSpec(memory_space=pltpu.SMEM)
HBM = pl.BlockSpec(memory_space=pltpu.HBM)
NT = (((1,), (1,)), ((), ()))


def chip_plan(count):
    first = sorted(range(1, count // 2), key=lambda g: (bin(g).count("1"), g))
    second = list(first)
    for n in range(0, len(first) - 1, 2):
        second[n], second[n + 1] = first[n + 1], first[n]
    return [*zip(first, second), (0, 0)]


def tile_plan(count):
    chips = chip_plan(count)[:-1]
    return [(2 * g + c, 2 * h + c) for c in (0, 1) for g, h in chips] + [(1, 1), (0, 0)]


def paired_plan(count):
    return [(2 * g, 2 * h) for g, h in chip_plan(count)]


def freq_plan(count):
    return [(d, d) for d in range(count - 1, -1, -1)]


def pick(pair, core):
    return pair[0] + core * (pair[1] - pair[0])


def came_from(step, core):
    return pick(step if step[0] % 2 == 0 else step[::-1], core)


def exchange(blocks, axis, plan):
    count = lax.axis_size(axis)
    return [
        lax.ppermute(x, axis, [(i, i ^ step[i % 2]) for i in range(count)]) if step[0] else x
        for x, step in zip(blocks, plan)
    ]


def analysis_kernel(dims, *refs):
    tile_count, outer, inner, rank_most, width, sources, conjugate, pieces, freqs, halves = dims
    ranks_ref, rows_ref, cols_ref, factors_ref = refs[:4]
    spectra_refs = refs[4 : 4 + pieces]
    out_count = tile_count if halves == 1 else 2 * halves
    out_refs = refs[4 + pieces : 4 + pieces + out_count]
    weights, *fetched = refs[4 + pieces + out_count :]
    per_dev = outer // tile_count
    lanes = 2 * sources // halves
    me = lax.axis_index("tile")
    core = me % 2
    chips = chip_plan(tile_count)
    firsts = [((me // 2) ^ pick(chip, core)) * 2 * per_dev for chip in chips]
    share = sources // freqs
    group = lax.axis_index("freq")
    plan = freq_plan(freqs)
    order = [pl.multiple_of((group ^ step[0]) * share, share) for step in plan]
    spots = order if halves == 1 else [n % (freqs // halves) * share for n in range(freqs)]

    if fetched:
        *tables, held, spectrum, sems = fetched
        moves = [(spectra_refs[0], spectrum), *zip((ranks_ref, rows_ref, cols_ref), tables)]
        for n, first in enumerate(firsts):
            place = pl.ds(n * 2 * per_dev, 2 * per_dev)
            moves.append((factors_ref.at[pl.ds(first, 2 * per_dev)], held.at[place]))
        copies = [pltpu.make_async_copy(x, y, sems.at[i]) for i, (x, y) in enumerate(moves)]
        for copy in copies:
            copy.start()
        for copy in copies[:4]:
            copy.wait()
        ranks_ref, rows_ref, cols_ref = tables
        spectra = [(spectrum[0, pl.ds(x, share)], spectrum[1, pl.ds(x, share)]) for x in order]
    else:
        spectra = [(ref[0], ref[1]) for ref in spectra_refs]
    for n, (real, imag) in enumerate(spectra):
        half, spot = n * halves // freqs, pl.ds(spots[n], share)
        weights[0, half, 0, spot] = real
        weights[0, half, 1, spot] = imag
        weights[1, half, 0, spot] = imag if conjugate else -imag
        weights[1, half, 1, spot] = -real if conjugate else real
    slots = lax.broadcasted_iota(jnp.int32, (rank_most, 2 * sources), 0)
    offsets = [core * per_dev, (1 - core) * per_dev]
    for n, first in enumerate(firsts):
        source, base = factors_ref, first
        if fetched:
            copies[4 + n].wait()
            source, base = held, n * 2 * per_dev
        for b in range(inner):
            span = slice(b * width, (b + 1) * width)
            here = me * inner + b
            total = None
            for p in range(2):
                factor = jnp.concatenate(
                    [
                        source[pl.ds(base + o, per_dev), p, :, span].reshape(-1, width)
                        for o in offsets
                    ]
                )
                weight = weights[p, :, :, :, span].reshape(2 * sources, width)
                term = lax.dot_general(factor, weight, NT, preferred_element_type=F32)
                total = term if total is None else total + term
            for c in (0, 1):
                for a in range(per_dev):
                    there = first + offsets[c] + a
                    row, col = (here, there) if conjugate else (there, here)
                    live = ranks_ref[rows_ref[row], cols_ref[col]]
                    at = (c * per_dev + a) * rank_most
                    part = jnp.where(slots < live, total[at : at + rank_most], 0.0).astype(BF16)
                    if halves == 1:
                        last = n == len(chips) - 1
                        step = tile_count - 1 - c if last else c * (len(chips) - 1) + n
                        out_refs[step][a, b] = part
                        continue
                    turn = n if c == 0 else chips.index(chips[n][::-1])
                    for h in range(halves):
                        out_refs[c * halves + h][turn, a, b] = part[:, h * lanes : (h + 1) * lanes]


def merge_kernel(inner, mine_ref, other_ref, *out_refs):
    core = lax.axis_index("tile") % 2
    for n, out_ref in enumerate(out_refs):
        out_ref[:, pl.ds(core * inner, inner)] = mine_ref[n]
        out_ref[:, pl.ds((1 - core) * inner, inner)] = other_ref[n]


def synthesis_kernel(dims, factors_ref, *refs):
    tile_count, outer, inner, rank_most, width, lanes, conjugate, paired, given, pieces, whole = dims
    plan = paired_plan(tile_count) if paired else tile_plan(tile_count)
    in_refs, refs = refs[: len(plan)], refs[len(plan) :]
    given_refs, refs = refs[:given], refs[given:]
    piece_refs, refs = refs[:pieces], refs[pieces:]
    held = refs[-1]
    me = lax.axis_index("tile")
    rows = outer // len(plan) * rank_most
    half = lanes // 2
    for ref, step in zip(in_refs, plan):
        source = me ^ came_from(step, me % 2)
        place = pl.multiple_of((source // 2 if paired else source) * rows, rows)
        for b in range(inner):
            held[b, pl.ds(place, rows)] = ref[b].reshape(rows, lanes)
    group = lax.axis_index("freq")
    for b in range(inner):
        span = slice(b * width, (b + 1) * width)
        turned = held[b].T
        by_real, by_imag = (
            jnp.dot(
                turned,
                factors_ref[:, p, :, span].reshape(outer * rank_most, width),
                preferred_element_type=F32,
            )
            for p in range(2)
        )
        if conjugate:
            real = by_real[:half] + by_imag[half:]
            imag = by_real[half:] - by_imag[:half]
        else:
            real = by_real[:half] - by_imag[half:]
            imag = by_real[half:] + by_imag[:half]
        real, imag = real.astype(BF16), imag.astype(BF16)
        if not pieces:
            refs[0][0, :, span] = real
            refs[0][1, :, span] = imag
        for n, ref in enumerate(piece_refs):
            share = half // pieces
            ref[0, :, span] = real[n * share : (n + 1) * share]
            ref[1, :, span] = imag[n * share : (n + 1) * share]
    if pieces and whole:
        parts = (*given_refs, *piece_refs)
        for ref, step in zip(parts, freq_plan(len(parts))):
            share = ref.shape[1]
            place = pl.multiple_of((group ^ step[0]) * share, share)
            refs[0][:, pl.ds(place, share)] = ref[...]


def gate_kernel(freqs, gate_ref, *refs):
    in_refs, out_refs = refs[:freqs], refs[freqs:]
    group = lax.axis_index("freq")
    parts = [(ref[0].astype(F32), ref[1].astype(F32)) for ref in in_refs]
    order = [step[0] for step in freq_plan(freqs)]
    for ref, d in zip(out_refs, order):
        target = group ^ d
        real = imag = None
        for (x, y), e in zip(parts, order):
            g = gate_ref[0, target, group ^ e]
            h = gate_ref[1, target, group ^ e]
            first = g * x - h * y
            second = g * y + h * x
            real = first if real is None else real + first
            imag = second if imag is None else imag + second
        ref[0] = real.astype(BF16)
        ref[1] = imag.astype(BF16)


def call(kernel, out_shape, specs, scratch, args, flops):
    held = sum(a.size * a.dtype.itemsize for a in args)
    held += sum(o.size * o.dtype.itemsize for o in out_shape)
    return pl.pallas_call(
        kernel,
        out_shape=out_shape,
        in_specs=specs,
        out_specs=[VMEM] * len(out_shape),
        scratch_shapes=scratch,
        compiler_params=pltpu.CompilerParams(vmem_limit_bytes=2 * held + (8 << 20)),
        cost_estimate=pl.CostEstimate(flops=flops, bytes_accessed=held, transcendentals=0),
    )(*args)


def shards(signal, v_factors, u_factors, tile_ranks, row_order, col_order, time_gate):
    tile_count = lax.axis_size("tile")
    freqs = lax.axis_size("freq")
    row_tiles, _, rank_most, col_local = v_factors.shape[1:]
    col_tiles = u_factors.shape[1]
    row_local = u_factors.shape[4]
    sources = signal.shape[2]
    col_dev = col_tiles // tile_count
    row_dev = row_tiles // tile_count
    width = col_local // col_dev
    share = sources // freqs
    flops = 8 * row_tiles * col_dev * rank_most * width * sources
    right, left = v_factors[0], u_factors[0]
    ranks = tile_ranks[0]

    def analysis(factors, spectra, outer, inner, conjugate, fetch, halves):
        per_dev = outer // tile_count
        pieces = len(spectra)
        dims = (
            (tile_count, outer, inner, rank_most, width, sources)
            + (conjugate, pieces, freqs, halves)
        )
        block = (per_dev, inner, rank_most, 2 * sources // halves)
        shapes = [jax.ShapeDtypeStruct(block, BF16)] * tile_count
        if halves > 1:
            shapes = [jax.ShapeDtypeStruct((tile_count // 2, *block), BF16)] * (2 * halves)
        tables = (ranks, row_order, col_order)
        specs = [SMEM] * 3 + [VMEM] * (1 + pieces)
        scratch = [pltpu.VMEM((2, halves, 2, sources // halves, inner * width), BF16)]
        if fetch:
            specs = [HBM] * (4 + pieces)
            scratch += [pltpu.SMEM(x.shape, x.dtype) for x in tables]
            scratch += [pltpu.VMEM(x.shape, x.dtype) for x in (factors, *spectra)]
            scratch += [pltpu.SemaphoreType.DMA((4 + tile_count // 2,))]
            tables = tuple(pltpu.with_memory_space_constraint(x, pltpu.HBM) for x in tables)
            factors = pltpu.with_memory_space_constraint(factors, pltpu.HBM)
            spectra = tuple(pltpu.with_memory_space_constraint(x, pltpu.HBM) for x in spectra)
        return call(
            functools.partial(analysis_kernel, dims),
            shapes,
            specs,
            scratch,
            (*tables, factors, *spectra),
            flops,
        )

    def merge(mine, other):
        _, per_dev, inner, _, lanes = mine.shape
        block = jax.ShapeDtypeStruct((per_dev, 2 * inner, rank_most, lanes), BF16)
        return call(
            functools.partial(merge_kernel, inner),
            [block] * mine.shape[0],
            [VMEM] * 2,
            [],
            (mine, other),
            0,
        )

    def synthesis(factors, blocks, outer, inner, conjugate, given, pieces, whole):
        lanes = blocks[0].shape[-1]
        dims = (
            (tile_count, outer, inner, rank_most, width, lanes, conjugate)
            + (len(blocks) < tile_count, len(given), pieces, whole)
        )
        shapes = [jax.ShapeDtypeStruct((2, share, inner * width), BF16)] * pieces
        if whole:
            shapes += [jax.ShapeDtypeStruct((2, sources, inner * width), BF16)]
        return call(
            functools.partial(synthesis_kernel, dims),
            shapes,
            [VMEM] * (1 + len(blocks) + len(given)),
            [pltpu.VMEM((inner, outer * rank_most, lanes), BF16)],
            (factors, *blocks, *given),
            flops * lanes // (2 * sources),
        )

    near, far = paired_plan(tile_count), freqs // 2
    *mine, first, second = analysis(right, (signal[0],), row_tiles, col_dev, False, True, 2)
    swap = [(i, i ^ 1) for i in range(tile_count)]
    swapped = [lax.ppermute(x, "tile", swap) for x in (first, second)]
    got = [exchange(merge(x, y), "tile", near) for x, y in zip(mine, swapped)]
    plan = freq_plan(freqs)
    pieces = synthesis(left, got[0], col_tiles, row_dev, False, (), far, False)
    come = exchange(pieces, "freq", plan[:far])
    *rest, forward = synthesis(left, got[1], col_tiles, row_dev, False, pieces, freqs - far, True)
    come += exchange(rest, "freq", plan[far:])
    gated = call(
        functools.partial(gate_kernel, freqs),
        [jax.ShapeDtypeStruct((2, share, row_local), BF16)] * freqs,
        [SMEM] + [VMEM] * freqs,
        [],
        (time_gate, *come),
        16 * freqs * freqs * share * row_local,
    )
    gated = exchange(gated, "freq", plan)
    sent = analysis(left, tuple(gated), col_tiles, row_dev, True, False, 1)
    got = exchange(sent, "tile", tile_plan(tile_count))
    (adjoint,) = synthesis(right, got, row_tiles, col_dev, True, (), 0, True)
    return forward[None], adjoint[None]


def solution(mesh):
    return jax.shard_map(
        shards,
        mesh=mesh,
        in_specs=(
            P("freq", None, None, "tile"),
            P("freq", None, None, None, "tile"),
            P("freq", None, None, None, "tile"),
            P("freq", None, None),
            P(),
            P(),
            P(),
        ),
        out_specs=(P("freq", None, None, "tile"), P("freq", None, None, "tile")),
        check_vma=False,
    )
```

```python
import functools

import jax
import jax.numpy as jnp
from jax import lax
from jax.experimental import pallas as pl
from jax.experimental.pallas import tpu as pltpu
from jax.sharding import PartitionSpec as P


F32 = jnp.float32
BF16 = jnp.bfloat16
VMEM = pl.BlockSpec(memory_space=pltpu.VMEM)
SMEM = pl.BlockSpec(memory_space=pltpu.SMEM)
HBM = pl.BlockSpec(memory_space=pltpu.HBM)
NT = (((1,), (1,)), ((), ()))


def chip_plan(count):
    first = sorted(range(1, count // 2), key=lambda g: (bin(g).count("1"), g))
    second = list(first)
    for n in range(0, len(first) - 1, 2):
        second[n], second[n + 1] = first[n + 1], first[n]
    return [*zip(first, second), (0, 0)]


def pick(pair, core):
    return pair[0] + core * (pair[1] - pair[0])


def tile_exchange(blocks):
    count = lax.axis_size("tile")
    steps = [(2 * g, 2 * h) for g, h in chip_plan(count)]
    return [
        lax.ppermute(x, "tile", [(i, i ^ step[i % 2]) for i in range(count)]) if step[0] else x
        for x, step in zip(blocks, steps)
    ]


def freq_exchange(blocks, steps):
    pairs = {d: [(i, i ^ d) for i in range(lax.axis_size("freq"))] for d in steps}
    return [lax.ppermute(x, "freq", pairs[d]) if d else x for x, d in zip(blocks, steps)]


def slice_of(step, share):
    return pl.ds(pl.multiple_of((lax.axis_index("freq") ^ step) * share, share), share)


def analysis_kernel(dims, *refs):
    tile_count, outer, inner, rank_most, width, conjugate, pieces, halves, steps = dims
    ranks_ref, rows_ref, cols_ref, factors_ref = refs[:4]
    spectra_refs = refs[4 : 4 + pieces]
    out_refs = refs[4 + pieces : 4 + pieces + 2 * halves]
    weights, *fetched = refs[4 + pieces + 2 * halves :]
    per_dev = outer // tile_count
    lanes = 2 * weights.shape[3]
    core = lax.axis_index("tile") % 2
    chip = lax.axis_index("tile") // 2
    chips = chip_plan(tile_count)
    firsts = [(chip ^ pick(step, core)) * 2 * per_dev for step in chips]

    if fetched:
        *tables, held, spectrum, sems = fetched
        moves = [(spectra_refs[0], spectrum), *zip((ranks_ref, rows_ref, cols_ref), tables)]
        for n, first in enumerate(firsts):
            place = pl.ds(n * 2 * per_dev, 2 * per_dev)
            moves.append((factors_ref.at[pl.ds(first, 2 * per_dev)], held.at[place]))
        copies = [pltpu.make_async_copy(x, y, sems.at[i]) for i, (x, y) in enumerate(moves)]
        for copy in copies:
            copy.start()
        for copy in copies[:4]:
            copy.wait()
        ranks_ref, rows_ref, cols_ref = tables
        share = spectrum.shape[1] // len(steps)
        spectra = [[spectrum[p, slice_of(d, share)] for p in range(2)] for d in steps]
    else:
        spectra = [(ref[0], ref[1]) for ref in spectra_refs]
    per_half = len(spectra) // halves
    for n, (real, imag) in enumerate(spectra):
        half, share = n // per_half, real.shape[0]
        spot = pl.ds(n % per_half * share, share)
        weights[0, half, 0, spot] = real
        weights[0, half, 1, spot] = imag
        weights[1, half, 0, spot] = imag if conjugate else -imag
        weights[1, half, 1, spot] = -real if conjugate else real
    slots = lax.broadcasted_iota(jnp.int32, (rank_most, halves * lanes), 0)
    offsets = [core * per_dev, (1 - core) * per_dev]
    for n, first in enumerate(firsts):
        source, base = factors_ref, first
        if fetched:
            copies[4 + n].wait()
            source, base = held, n * 2 * per_dev
        for b in range(inner):
            span = slice(b * width, (b + 1) * width)
            here = lax.axis_index("tile") * inner + b
            total = None
            for p in range(2):
                factor = jnp.concatenate(
                    [
                        source[pl.ds(base + o, per_dev), p, :, span].reshape(-1, width)
                        for o in offsets
                    ]
                )
                weight = weights[p, :, :, :, span].reshape(halves * lanes, width)
                term = lax.dot_general(factor, weight, NT, preferred_element_type=F32)
                total = term if total is None else total + term
            for c in (0, 1):
                turn = n if c == 0 else chips.index(chips[n][::-1])
                for a in range(per_dev):
                    there = first + offsets[c] + a
                    row, col = (here, there) if conjugate else (there, here)
                    live = ranks_ref[rows_ref[row], cols_ref[col]]
                    at = (c * per_dev + a) * rank_most
                    part = jnp.where(slots < live, total[at : at + rank_most], 0.0).astype(BF16)
                    for h in range(halves):
                        out_refs[c * halves + h][turn, a, b] = part[:, h * lanes : (h + 1) * lanes]


def merge_kernel(inner, mine_ref, other_ref, *out_refs):
    core = lax.axis_index("tile") % 2
    for n, out_ref in enumerate(out_refs):
        out_ref[:, pl.ds(core * inner, inner)] = mine_ref[n]
        out_ref[:, pl.ds((1 - core) * inner, inner)] = other_ref[n]


def synthesis_kernel(dims, factors_ref, *refs):
    tile_count, outer, inner, rank_most, width, conjugate, steps, given = dims
    chips = chip_plan(tile_count)
    in_refs, refs = refs[: len(chips)], refs[len(chips) :]
    given_refs, out_refs, held = refs[: len(given)], refs[len(given) : -1], refs[-1]
    core = lax.axis_index("tile") % 2
    chip = lax.axis_index("tile") // 2
    rows = outer // len(chips) * rank_most
    lanes = held.shape[-1]
    half = lanes // 2
    share = half // len(steps)
    for ref, step in zip(in_refs, chips):
        place = pl.multiple_of((chip ^ pick(step, core)) * rows, rows)
        for b in range(inner):
            held[b, pl.ds(place, rows)] = ref[b].reshape(rows, lanes)
    for ref, step in zip(given_refs, given):
        out_refs[0][:, slice_of(step, share)] = ref[...]
    for b in range(inner):
        span = slice(b * width, (b + 1) * width)
        turned = held[b].T
        by_real, by_imag = (
            jnp.dot(
                turned,
                factors_ref[:, p, :, span].reshape(outer * rank_most, width),
                preferred_element_type=F32,
            )
            for p in range(2)
        )
        if conjugate:
            real = by_real[:half] + by_imag[half:]
            imag = by_real[half:] - by_imag[:half]
        else:
            real = by_real[:half] - by_imag[half:]
            imag = by_real[half:] + by_imag[:half]
        for p, part in enumerate((real.astype(BF16), imag.astype(BF16))):
            for n, step in enumerate(steps):
                piece = part[n * share : (n + 1) * share]
                if given:
                    out_refs[0][p, slice_of(step, share), span] = piece
                else:
                    out_refs[n][p, :, span] = piece


def collect_kernel(steps, *refs):
    for ref, step in zip(refs, steps):
        refs[-1][:, slice_of(step, ref.shape[1])] = ref[...]


def gate_kernel(takes, sends, gate_ref, *refs):
    in_refs, out_refs = refs[: len(takes)], refs[len(takes) :]
    group = lax.axis_index("freq")
    parts = [(ref[0].astype(F32), ref[1].astype(F32)) for ref in in_refs]
    for ref, d in zip(out_refs, sends):
        target = group ^ d
        real = imag = None
        for (x, y), e in zip(parts, takes):
            g = gate_ref[0, target, group ^ e]
            h = gate_ref[1, target, group ^ e]
            first = g * x - h * y
            second = g * y + h * x
            real = first if real is None else real + first
            imag = second if imag is None else imag + second
        ref[0] = real.astype(BF16)
        ref[1] = imag.astype(BF16)


def call(kernel, out_shape, specs, scratch, args, flops):
    held = sum(a.size * a.dtype.itemsize for a in args)
    held += sum(o.size * o.dtype.itemsize for o in out_shape)
    return pl.pallas_call(
        kernel,
        out_shape=out_shape,
        in_specs=specs,
        out_specs=[VMEM] * len(out_shape),
        scratch_shapes=scratch,
        compiler_params=pltpu.CompilerParams(vmem_limit_bytes=2 * held + (8 << 20)),
        cost_estimate=pl.CostEstimate(flops=flops, bytes_accessed=held, transcendentals=0),
    )(*args)


def shards(signal, v_factors, u_factors, tile_ranks, row_order, col_order, time_gate):
    tile_count = lax.axis_size("tile")
    freqs = lax.axis_size("freq")
    row_tiles, _, rank_most, col_local = v_factors.shape[1:]
    col_tiles = u_factors.shape[1]
    row_local = u_factors.shape[4]
    sources = signal.shape[2]
    col_dev = col_tiles // tile_count
    row_dev = row_tiles // tile_count
    width = col_local // col_dev
    share = sources // freqs
    flops = 8 * row_tiles * col_dev * rank_most * width * sources
    right, left = v_factors[0], u_factors[0]
    ranks = tile_ranks[0]

    def analysis(factors, spectra, outer, inner, conjugate, steps, halves, fetch):
        per_dev = outer // tile_count
        here = share * len(steps)
        dims = (tile_count, outer, inner, rank_most, width, conjugate, len(spectra), halves, steps)
        block = (tile_count // 2, per_dev, inner, rank_most, 2 * here // halves)
        tables = (ranks, row_order, col_order)
        specs = [SMEM] * 3 + [VMEM] * (1 + len(spectra))
        scratch = [pltpu.VMEM((2, halves, 2, here // halves, inner * width), BF16)]
        if fetch:
            specs = [HBM] * (4 + len(spectra))
            scratch += [pltpu.SMEM(x.shape, x.dtype) for x in tables]
            scratch += [pltpu.VMEM(x.shape, x.dtype) for x in (factors, *spectra)]
            scratch += [pltpu.SemaphoreType.DMA((4 + tile_count // 2,))]
            tables = tuple(pltpu.with_memory_space_constraint(x, pltpu.HBM) for x in tables)
            factors = pltpu.with_memory_space_constraint(factors, pltpu.HBM)
            spectra = tuple(pltpu.with_memory_space_constraint(x, pltpu.HBM) for x in spectra)
        return call(
            functools.partial(analysis_kernel, dims),
            [jax.ShapeDtypeStruct(block, BF16)] * (2 * halves),
            specs,
            scratch,
            (*tables, factors, *spectra),
            flops * len(steps) // freqs,
        )

    def merge(mine, other):
        _, per_dev, inner, _, lanes = mine.shape
        block = jax.ShapeDtypeStruct((per_dev, 2 * inner, rank_most, lanes), BF16)
        return call(
            functools.partial(merge_kernel, inner),
            [block] * mine.shape[0],
            [VMEM] * 2,
            [],
            (mine, other),
            0,
        )

    def synthesis(factors, blocks, outer, inner, conjugate, steps, given=(), ready=()):
        dims = (tile_count, outer, inner, rank_most, width, conjugate, steps, given)
        lanes = blocks[0].shape[-1]
        shapes = [jax.ShapeDtypeStruct((2, share, inner * width), BF16)] * len(steps)
        if given:
            shapes = [jax.ShapeDtypeStruct((2, sources, inner * width), BF16)]
        return call(
            functools.partial(synthesis_kernel, dims),
            shapes,
            [VMEM] * (1 + len(blocks) + len(ready)),
            [pltpu.VMEM((inner, outer * rank_most, lanes), BF16)],
            (factors, *blocks, *ready),
            flops * len(steps) // freqs,
        )

    def swap(x):
        return lax.ppermute(x, "tile", [(i, i ^ 1) for i in range(tile_count)])

    far = tuple(range(freqs - 1, freqs // 2 - 1, -1))
    near = tuple(range(freqs // 2 - 1, -1, -1))
    mine_far, mine_near, give_far, give_near = analysis(
        right, (signal[0],), row_tiles, col_dev, False, far + near, 2, True
    )
    give_far, give_near = swap(give_far), swap(give_near)
    got_far = tile_exchange(merge(mine_far, give_far))
    got_near = tile_exchange(merge(mine_near, give_near))
    done_far = synthesis(left, got_far, col_tiles, row_dev, False, far)
    come_far = freq_exchange(done_far, far)
    done_near = synthesis(left, got_near, col_tiles, row_dev, False, near)
    come_near = freq_exchange(done_near, near)
    (forward,) = call(
        functools.partial(collect_kernel, far + near),
        [jax.ShapeDtypeStruct((2, sources, row_local), BF16)],
        [VMEM] * freqs,
        [],
        (*done_far, *done_near),
        0,
    )
    sends = near[:-1] + far + near[-1:]
    gated = call(
        functools.partial(gate_kernel, far + near, sends),
        [jax.ShapeDtypeStruct((2, share, row_local), BF16)] * freqs,
        [SMEM] + [VMEM] * freqs,
        [],
        (time_gate, *come_far, *come_near),
        16 * freqs * freqs * share * row_local,
    )
    gated = dict(zip(sends, gated))
    back_near = freq_exchange([gated[d] for d in near], near)
    back_far = freq_exchange([gated[d] for d in far], far)
    mine_near, give_near = analysis(
        left, tuple(back_near), col_tiles, row_dev, True, near, 1, False
    )
    give_near = swap(give_near)
    merged = merge(mine_near, give_near)
    got_near = tile_exchange(merged)
    mine_far, give_far = analysis(left, tuple(back_far), col_tiles, row_dev, True, far, 1, False)
    give_far = swap(give_far)
    merged = merge(mine_far, give_far)
    got_far = tile_exchange(merged)
    ready = synthesis(right, got_near, row_tiles, col_dev, True, near)
    (adjoint,) = synthesis(right, got_far, row_tiles, col_dev, True, far, near, ready)
    return forward[None], adjoint[None]


def solution(mesh):
    return jax.shard_map(
        shards,
        mesh=mesh,
        in_specs=(
            P("freq", None, None, "tile"),
            P("freq", None, None, None, "tile"),
            P("freq", None, None, None, "tile"),
            P("freq", None, None),
            P(),
            P(),
            P(),
        ),
        out_specs=(P("freq", None, None, "tile"), P("freq", None, None, "tile")),
        check_vma=False,
    )
```
